32 devices in a mesh: ctx: 8 (over z, x), head: 4 (over y, core).
Axes of the slice: x: 2, y: 2, z: 4, core: 2. Of those that a mesh axis runs over, the one named last changes fastest.
Arguments:
- queries: bfloat16 [4096, 3072], P('ctx', 'head'), may hold values from -26 to 26
- keys: bfloat16 [4096, 3072], P('ctx', 'head'), may hold values from -26 to 26
- values: bfloat16 [4096, 3072], P('ctx', 'head'), may hold values from -6 to 6
- kv_tiles: int32 [32, 12], replicated, may hold values from 0 to 31, as said below
- out_weight: bfloat16 [3072, 3072], P('head'), may hold values from -0.109375 to 0.109375
Outputs:
- attended: bfloat16 [4096, 3072], P(('ctx', 'head'))
The draws below stay inside these ranges and needn't reach their ends.
Inputs may be any that keep to these rules, and one draw needn't show every extreme that they name: `kv_tiles`: every row i lists tile i itself; entries may repeat. A listed tile lies on a device (tile index // 4) within 2 of the device of row i, and from every other device within 2 the rows of one device read between 1 and 2 distinct tiles.
All inputs are finite; a program needn't handle non-finite values.
Results may differ from the reference program's by a relative error of at most 0.009.
Values may be sent and summed in bfloat16 or wider, within the bound.
A program may use at most 128 MiB of HBM per device.

```python
import jax
import jax.numpy as jnp
from jax import lax

HEADS = 24
HD = 128
DOUT = 3072
TILE = 128
REACH = 2
CAP = 2
QT = 4
NT = 32
MAXK = 12
TOKENS = 4096
N_HEAD = 4


def draw_queries(key, part):
    shape = (TOKENS, HEADS * HD)
    base = jnp.clip(jax.random.normal(jax.random.fold_in(key, 1), shape, dtype=jnp.float32), -4.0, 4.0)
    return base.astype(jnp.bfloat16)


def draw_keys(key, part):
    shape = (TOKENS, HEADS * HD)
    base = jnp.clip(jax.random.normal(jax.random.fold_in(key, 2), shape, dtype=jnp.float32), -4.0, 4.0)
    return base.astype(jnp.bfloat16)


def draw_kv_tiles(key, part):
    dev_count = NT // QT
    offsets = jnp.arange(2 * REACH, dtype=jnp.int32)
    offsets = jnp.where(offsets < REACH, offsets - REACH, offsets - REACH + 1)
    devices = jnp.arange(dev_count, dtype=jnp.int32)
    sources = devices[:, None] + offsets[None, :]
    in_range = (sources >= 0) & (sources < dev_count)
    heavy = jax.random.randint(jax.random.fold_in(key, 1), (dev_count, 2 * REACH), 0, 4, dtype=jnp.int32) == 0
    needed = jnp.where(heavy, CAP, 1)
    busiest = jax.random.randint(jax.random.fold_in(key, 2), (), 0, dev_count, dtype=jnp.int32)
    needed = jnp.where(devices[:, None] == busiest, CAP, needed)
    tile_local = jnp.arange(QT, dtype=jnp.int32)
    ranking = jax.random.randint(jax.random.fold_in(key, 3), (dev_count, 2 * REACH, QT), 0, 1048576, dtype=jnp.int32) * QT + tile_local
    picked = jnp.argsort(ranking, axis=-1)[:, :, :CAP].astype(jnp.int32)
    slot_ids = jnp.arange(CAP, dtype=jnp.int32)
    remote_usable = in_range[:, :, None] & (slot_ids[None, None, :] < needed[:, :, None])
    remote_ids = sources[:, :, None] * QT + picked
    own_ids = devices[:, None] * QT + tile_local[None, :]
    candidates = jnp.concatenate([own_ids, remote_ids.reshape(dev_count, 2 * REACH * CAP)], axis=1)
    usable = jnp.concatenate([jnp.ones((dev_count, QT), dtype=bool), remote_usable.reshape(dev_count, 2 * REACH * CAP)], axis=1)
    primary = jax.random.randint(jax.random.fold_in(key, 4), (dev_count, MAXK), 0, QT, dtype=jnp.int32)
    second = jax.random.randint(jax.random.fold_in(key, 5), (dev_count, MAXK), 0, 2, dtype=jnp.int32) == 1
    assigned = (primary[:, None, :] == tile_local[None, :, None]) | second[:, None, :] & (((primary + 1) % QT)[:, None, :] == tile_local[None, :, None])
    diagonal = devices[:, None] * QT + tile_local[None, :]
    entries = jnp.where(usable[:, None, :] & assigned, candidates[:, None, :], diagonal[:, :, None])
    shuffle = jax.random.randint(jax.random.fold_in(key, 6), (dev_count, QT, MAXK), 0, 1048576, dtype=jnp.int32) * MAXK + jnp.arange(MAXK, dtype=jnp.int32)
    permuted_at = jnp.argsort(shuffle, axis=-1)
    entries = jnp.take_along_axis(entries, permuted_at, axis=-1)
    return entries.reshape(NT, MAXK).astype(jnp.int32)


def block_scale(rng, extent, pieces, least, high):
    gain = 1.0
    for axis_at, blocks in pieces:
        steps = jax.random.uniform(jax.random.fold_in(jax.random.fold_in(rng, 6), axis_at), (blocks,), jnp.float32, least / len(pieces), high / len(pieces))
        gain = gain * jnp.repeat(jnp.exp(steps), extent[axis_at] // blocks).reshape((-1,) + (1,) * (len(extent) - 1 - axis_at))
    return gain


def gaussian(key, shape, width, bound, pieces=(), held_as=jnp.bfloat16):
    factor_of = block_scale(key, shape, pieces, -0.22, 0.18) if pieces else 1.0
    values = jax.random.normal(key, shape, jnp.float32) * width * factor_of
    return jnp.minimum(jnp.maximum(values, -bound), bound).astype(held_as)


def setup_inputs(seed: int = 0) -> dict:
    seeds = jax.random.split(jax.random.key(seed), 6)
    return {
        "queries": draw_queries(jax.random.fold_in(seeds[5], 71), 0),
        "keys": draw_keys(jax.random.fold_in(seeds[5], 71), 0),
        "values": gaussian(seeds[2], (TOKENS, HEADS * HD), 1.0, 6.0, ((0, 8), (1, 4))),
        "kv_tiles": draw_kv_tiles(jax.random.fold_in(seeds[5], 71), 0),
        "out_weight": gaussian(seeds[4], (HEADS * HD, DOUT), (HEADS * HD) ** -0.5, 0.109375, ((0, 4),)),
    }


def reference(queries, keys, values, kv_tiles, out_weight):
    query_tiles = queries.reshape(NT, TILE, HEADS, HD)
    key_tiles = keys.reshape(NT, TILE, HEADS * HD)
    value_tiles = values.reshape(NT, TILE, HEADS * HD)
    earlier = jnp.tril(jnp.ones((MAXK, MAXK), dtype=bool), -1)
    score_scale = HD ** -0.5

    def one_tile(tile_index):
        tile_list = kv_tiles[tile_index]
        repeated = jnp.any((tile_list[:, None] == tile_list[None, :]) & earlier, axis=1)
        key_rows = key_tiles[tile_list].reshape(MAXK * TILE, HEADS, HD).astype(jnp.float32)
        value_rows = value_tiles[tile_list].reshape(MAXK * TILE, HEADS, HD).astype(jnp.float32)
        query_rows = query_tiles[tile_index].astype(jnp.float32)
        scores = jnp.einsum("qhd,khd->hqk", query_rows, key_rows) * score_scale
        allowed = jnp.repeat(jnp.logical_not(repeated), TILE)[None, None, :]
        masked = jnp.where(allowed, scores, -jnp.inf)
        row_max = jnp.max(masked, axis=-1, keepdims=True)
        weights = jnp.where(allowed, jnp.exp(masked - row_max), 0.0)
        denominator = jnp.sum(weights, axis=-1)
        rounded = lax.optimization_barrier(weights.astype(jnp.bfloat16)).astype(jnp.float32)
        summed = jnp.einsum("hqk,khd->qhd", rounded, value_rows)
        context_rows = summed / jnp.transpose(denominator)[:, :, None]
        return context_rows.astype(jnp.bfloat16).reshape(TILE, HEADS * HD)

    context = lax.map(one_tile, jnp.arange(NT, dtype=jnp.int32)).reshape(TOKENS, HEADS * HD)
    group_width = HEADS * HD // N_HEAD
    summed_out = jnp.zeros((TOKENS, DOUT), jnp.float32)
    for group_index in range(N_HEAD):
        lower = group_index * group_width
        partial_value = jnp.dot(context[:, lower:lower + group_width], out_weight[lower:lower + group_width], preferred_element_type=jnp.float32).astype(jnp.bfloat16)
        summed_out = summed_out + partial_value.astype(jnp.float32)
    return summed_out.astype(jnp.bfloat16)
```

```python
import jax
import jax.numpy as jnp
from jax import lax
from jax.sharding import PartitionSpec as P

HD = 128
TILE = 128
REACH = 2
PAIR = 2


def shifted(value, axis, by):
    peers = lax.axis_size(axis)
    pairs = [(i, i + by) for i in range(peers) if 0 <= i + by < peers]
    return lax.ppermute(value, axis, pairs)


def extremes(kv_tiles, reader, owner, per, devices):
    rows = lax.dynamic_slice_in_dim(kv_tiles, jnp.clip(reader, 0, devices - 1) * per, per, 0)
    inside = (rows // per == owner) & (reader >= 0) & (reader < devices)
    least = jnp.min(jnp.where(inside, rows % per, per - 1))
    most = jnp.max(jnp.where(inside, rows % per, 0))
    return least, most, jnp.any(inside)


def body(queries, keys, values, kv_tiles, out_weight):
    tok_rows, columns = queries.shape
    heads_here = columns // HD
    per = tok_rows // TILE
    device = lax.axis_index("ctx")
    devices = lax.axis_size("ctx")
    stacked = jnp.stack([keys, values])
    pieces = [stacked]
    id_parts = [device * per + jnp.arange(per, dtype=jnp.int32)]
    for offset in [o for o in range(-REACH, REACH + 1) if o]:
        least, most, _ = extremes(kv_tiles, device - offset, device, per, devices)
        packed = jnp.concatenate(
            [lax.dynamic_slice_in_dim(stacked, t * TILE, TILE, 1) for t in (least, most)], axis=1
        )
        pieces.append(shifted(packed, "ctx", -offset))
        source = device + offset
        least, most, found = extremes(kv_tiles, device, source, per, devices)
        id_parts.append(
            jnp.stack([
                jnp.where(found, source * per + least, -1),
                jnp.where(found & (most != least), source * per + most, -1),
            ])
        )
    buffer = jnp.concatenate(pieces, axis=1)
    tile_ids = jnp.concatenate(id_parts)
    key_tiles = tile_ids.shape[0]
    own_lists = lax.dynamic_slice_in_dim(kv_tiles, device * per, per, 0)
    allowed = jnp.any(own_lists[:, None, :] == tile_ids[None, :, None], axis=2)
    allowed_keys = jnp.broadcast_to(
        allowed[:, None, :, None], (per, TILE, key_tiles, TILE)
    ).reshape(tok_rows, key_tiles * TILE)
    query_heads = queries.reshape(tok_rows, heads_here, HD)
    key_heads = buffer[0].reshape(key_tiles * TILE, heads_here, HD)
    value_heads = buffer[1].reshape(key_tiles * TILE, heads_here, HD)
    scores = jnp.einsum(
        "qhd,khd->hqk", query_heads, key_heads, preferred_element_type=jnp.float32
    ) * HD ** (-0.5)
    masked = jnp.where(allowed_keys[None], scores, -jnp.inf)
    row_max = jnp.max(masked, axis=-1, keepdims=True)
    weights = jnp.where(allowed_keys[None], jnp.exp(masked - row_max), 0.0)
    denominator = jnp.sum(weights, axis=-1)
    rounded = weights.astype(jnp.bfloat16)
    summed = jnp.einsum("hqk,khd->qhd", rounded, value_heads, preferred_element_type=jnp.float32)
    context = (
        (summed / jnp.transpose(denominator)[:, :, None])
        .astype(jnp.bfloat16)
        .reshape(tok_rows, columns)
    )
    return lax.psum_scatter(
        jnp.dot(context, out_weight, preferred_element_type=jnp.float32).astype(jnp.bfloat16),
        "head",
        scatter_dimension=0,
        tiled=True,
    )


def solution(mesh):
    return jax.shard_map(
        body,
        mesh=mesh,
        in_specs=(P("ctx", "head"), P("ctx", "head"), P("ctx", "head"), P(), P("head", None)),
        out_specs=P(("ctx", "head"), None),
        check_vma=False,
    )
```

```python
import functools
import math

import jax
import jax.numpy as jnp
from jax import lax
from jax.experimental import pallas as pl
from jax.experimental.pallas import tpu as pltpu
from jax.sharding import PartitionSpec as P

HD = 128
TILE = 128
REACH = 2
PAIR = 2
OFFSETS = tuple(o for o in range(-REACH, REACH + 1) if o)
MASKED = -1e30
MESH = pl.DeviceIdType.MESH


def dot(a, b, contract):
    return lax.dot_general(a, b, (((1,), (contract,)), ((), ())), preferred_element_type=jnp.float32)


def kernel(devices, groups, chunk, ids, bias, q, k, v, w, out,
           packed, halo, ctx, ctx_mate, w_own, w_mate, part_out, part_in, own,
           halo_send, halo_recv, ctx_send, ctx_recv, part_send, part_recv, w_sems):
    device, group = lax.axis_index("ctx"), lax.axis_index("head")
    parity, place = group % 2, group // 2
    mate = group + 1 - 2 * parity
    tokens, columns = q.shape
    heads, tiles = columns // HD, tokens // TILE
    width = out.shape[1]
    rows = tokens // groups
    pairs = groups // 2
    chunks = width // chunk

    def reader(slot):
        return device - OFFSETS[slot]

    def source(slot):
        return device + OFFSETS[slot]

    def inside(index):
        return (index >= 0) & (index < devices)

    barrier = pltpu.get_barrier_semaphore()
    expected = jnp.int32(pairs)
    for slot in range(len(OFFSETS)):
        @pl.when(inside(reader(slot)))
        def _(slot=slot):
            pl.semaphore_signal(barrier, 1, device_id=(reader(slot), group), device_id_type=MESH)
        expected = expected + inside(source(slot)).astype(jnp.int32)
    pl.semaphore_signal(barrier, 1, device_id=(device, mate), device_id_type=MESH)
    for step in range(1, pairs):
        peer = 2 * ((place + step) % pairs) + parity
        pl.semaphore_signal(barrier, 1, device_id=(device, peer), device_id_type=MESH)

    load_w = pltpu.make_async_copy(w, w_own, w_sems.at[0])
    load_w.start()

    for slot in range(len(OFFSETS)):
        for which in range(PAIR):
            picked = ids[PAIR * slot + which]
            for side, ref in ((0, k), (1, v)):
                tile = ref[picked]
                for h in range(heads):
                    packed[h, slot, side, which * TILE:(which + 1) * TILE, :] = tile[:, h * HD:(h + 1) * HD]
    for slot in range(len(OFFSETS)):
        @pl.when(jnp.logical_not(inside(source(slot))))
        def _(slot=slot):
            halo[:, :, slot] = jnp.zeros((heads, 2, PAIR * TILE, HD), halo.dtype)

    pl.semaphore_wait(barrier, expected)

    def halo_copy(h, slot):
        return pltpu.make_async_remote_copy(
            src_ref=packed.at[h, slot], dst_ref=halo.at[h, :, slot],
            send_sem=halo_send.at[h, slot], recv_sem=halo_recv.at[h, slot],
            device_id=(reader(slot), group), device_id_type=MESH)

    def each_send(act):
        def one(h, carry):
            for slot in range(len(OFFSETS)):
                @pl.when(inside(reader(slot)))
                def _(slot=slot):
                    act(halo_copy(h, slot))
            return carry
        lax.fori_loop(0, heads, one, 0)

    each_send(lambda copy: copy.start())
    send_w = pltpu.make_async_remote_copy(
        src_ref=w, dst_ref=w_mate, send_sem=w_sems.at[1], recv_sem=w_sems.at[2],
        device_id=(device, mate), device_id_type=MESH)
    send_w.start()

    def ctx_copy(h, i):
        block = pl.multiple_of((2 * i + 1 - parity) * rows, rows)
        lanes = pl.ds(pl.multiple_of(h * HD, HD), HD)
        return pltpu.make_async_remote_copy(
            src_ref=ctx.at[pl.ds(block, rows), lanes],
            dst_ref=ctx_mate.at[pl.ds(i * rows, rows), lanes],
            send_sem=ctx_send.at[h, i], recv_sem=ctx_recv.at[h, i],
            device_id=(device, mate), device_id_type=MESH)

    scale = HD ** -0.5 * math.log2(math.e)
    near = tokens

    def one_head(h, carry):
        for slot in range(len(OFFSETS)):
            @pl.when(inside(source(slot)))
            def _(slot=slot):
                halo_copy(h, slot).wait_recv()
        lanes = pl.ds(pl.multiple_of(h * HD, HD), HD)
        k_own, v_own = k[:, :, lanes].reshape(tokens, HD), v[:, :, lanes].reshape(tokens, HD)
        k_far = halo[h, 0].reshape(len(OFFSETS) * PAIR * TILE, HD)
        v_far = halo[h, 1].reshape(len(OFFSETS) * PAIR * TILE, HD)
        for i in range(tiles):
            half = tiles // 2
            t = 2 * i + 1 - parity if i < half else 2 * (i - half) + parity
            span = pl.ds(pl.multiple_of(t * TILE, TILE), TILE)
            qt = q[span, lanes]
            shift = bias[pl.ds(t, 1), :]
            s_own = dot(qt, k_own, 1) * scale + shift[:, :near]
            s_far = dot(qt, k_far, 1) * scale + shift[:, near:]
            top = jnp.maximum(jnp.max(s_own, axis=1, keepdims=True), jnp.max(s_far, axis=1, keepdims=True))
            p_own, p_far = jnp.exp2(s_own - top), jnp.exp2(s_far - top)
            total = jnp.sum(p_own, axis=1, keepdims=True) + jnp.sum(p_far, axis=1, keepdims=True)
            summed = dot(p_own.astype(jnp.bfloat16), v_own, 0) + dot(p_far.astype(jnp.bfloat16), v_far, 0)
            ctx[span, lanes] = (summed * (1.0 / total)).astype(ctx.dtype)
            if i == (half if rows == TILE and half < tiles else tiles - 1):
                for j in range(pairs):
                    ctx_copy(h, j).start()
        return carry

    lax.fori_loop(0, heads, one_head, 0)

    load_w.wait()
    send_w.wait_recv()

    def wait_ctx(h, carry):
        for j in range(pairs):
            ctx_copy(h, j).wait_recv()
        return carry
    lax.fori_loop(0, heads, wait_ctx, 0)

    def project(i, c):
        mine = ctx[pl.ds(pl.multiple_of((2 * i + parity) * rows, rows), rows), :]
        other = ctx_mate[pl.ds(pl.multiple_of(i * rows, rows), rows), :]
        cols = pl.ds(c * chunk, chunk)
        return dot(mine, w_own[:, cols], 0) + dot(other, w_mate[:, cols], 0)

    def part_copy(step, c):
        peer = 2 * ((place + step) % pairs) + parity
        cols = pl.ds(c * chunk, chunk)
        return pltpu.make_async_remote_copy(
            src_ref=part_out.at[step - 1, c], dst_ref=part_in.at[step - 1, c],
            send_sem=part_send.at[step - 1, c], recv_sem=part_recv.at[step - 1, c],
            device_id=(device, peer), device_id_type=MESH)

    waiting = None
    for step in range(1, pairs):
        for c in range(chunks):
            part_out[step - 1, c] = project((place + step) % pairs, c).astype(part_out.dtype)
            if waiting is not None:
                part_copy(*waiting).start()
            waiting = (step, c)
    for c in range(chunks):
        own[c] = project(place, c)
        if waiting is not None:
            part_copy(*waiting).start()
            waiting = None
    for c in range(chunks):
        total = own[c]
        for step in range(1, pairs):
            part_copy(step, c).wait_recv()
            total = total + part_in[step - 1, c].astype(jnp.float32)
        out[:, c * chunk:(c + 1) * chunk] = total.astype(out.dtype)

    each_send(lambda copy: copy.wait_send())
    send_w.wait_send()

    def drain_ctx(h, carry):
        for j in range(pairs):
            ctx_copy(h, j).wait_send()
        return carry
    lax.fori_loop(0, heads, drain_ctx, 0)
    for step in range(1, pairs):
        for c in range(chunks):
            part_copy(step, c).wait_send()


def plan(kv_tiles, per):
    device = lax.axis_index("ctx")
    shifts = jnp.array(OFFSETS, jnp.int32)
    near = jnp.full_like(shifts, device)
    readers = jnp.concatenate([device - shifts, near])[:, None, None]
    owners = jnp.concatenate([near, device + shifts])[:, None, None]
    home = lax.broadcasted_iota(jnp.int32, kv_tiles.shape, 0) // per
    local = kv_tiles % per
    read = (home == readers) & (kv_tiles // per == owners)
    least = jnp.min(jnp.where(read, local, per), axis=(1, 2))
    most = jnp.max(jnp.where(read, local, -1), axis=(1, 2))
    count = len(OFFSETS)
    ids = jnp.stack([jnp.minimum(least[:count], per - 1), jnp.maximum(most[:count], 0)], axis=1)
    least, most, base = least[count:], most[count:], (device + shifts) * per
    far = jnp.stack(
        [jnp.where(least < per, base + least, -1), jnp.where(most > least, base + most, -1)], axis=1
    )
    listed = jnp.concatenate([device * per + jnp.arange(per, dtype=jnp.int32), far.reshape(-1)])
    mine = lax.dynamic_slice_in_dim(kv_tiles, device * per, per, 0)
    allowed = jnp.any(mine[:, None, :] == listed[None, :, None], axis=2)
    bias = jnp.where(allowed, 0.0, MASKED).astype(jnp.float32)
    bias = jnp.broadcast_to(bias[:, :, None], bias.shape + (TILE,)).reshape(per, -1)
    return ids.reshape(-1), bias


def body(queries, keys, values, kv_tiles, out_weight):
    tokens, columns = queries.shape
    width = out_weight.shape[1]
    devices, groups = lax.axis_size("ctx"), lax.axis_size("head")
    heads, rows, pairs, slots = columns // HD, tokens // groups, groups // 2, len(OFFSETS)
    chunk = min(width, 512)
    chunks = width // chunk
    ids, bias = plan(kv_tiles, tokens // TILE)
    vmem = pl.BlockSpec(memory_space=pltpu.VMEM)
    sems = pltpu.SemaphoreType.DMA
    bf16 = jnp.bfloat16
    return pl.pallas_call(
        functools.partial(kernel, devices, groups, chunk),
        out_shape=jax.ShapeDtypeStruct((rows, width), bf16),
        in_specs=[pl.BlockSpec(memory_space=pltpu.SMEM), vmem, vmem, vmem, vmem,
                  pl.BlockSpec(memory_space=pl.ANY)],
        out_specs=vmem,
        scratch_shapes=[
            pltpu.VMEM((heads, slots, 2, PAIR * TILE, HD), bf16),
            pltpu.VMEM((heads, 2, slots, PAIR * TILE, HD), bf16),
            pltpu.VMEM((tokens, columns), bf16),
            pltpu.VMEM((pairs * rows, columns), bf16),
            pltpu.VMEM((columns, width), bf16),
            pltpu.VMEM((columns, width), bf16),
            pltpu.VMEM((pairs - 1, chunks, rows, chunk), bf16),
            pltpu.VMEM((pairs - 1, chunks, rows, chunk), bf16),
            pltpu.VMEM((chunks, rows, chunk), jnp.float32),
            sems((heads, slots)), sems((heads, slots)),
            sems((heads, pairs)), sems((heads, pairs)),
            sems((pairs - 1, chunks)), sems((pairs - 1, chunks)),
            sems((3,)),
        ],
        compiler_params=pltpu.CompilerParams(
            collective_id=0, has_side_effects=True, vmem_limit_bytes=56 * 2 ** 20),
    )(ids, bias, queries, keys.reshape(-1, TILE, columns), values.reshape(-1, TILE, columns), out_weight)


def solution(mesh):
    return jax.shard_map(
        body,
        mesh=mesh,
        in_specs=(P("ctx", "head"), P("ctx", "head"), P("ctx", "head"), P(), P("head", None)),
        out_specs=P(("ctx", "head"), None),
        check_vma=False,
    )
```

```python
import functools
import math

import jax
import jax.numpy as jnp
from jax import lax
from jax.experimental import pallas as pl
from jax.experimental.pallas import tpu as pltpu
from jax.sharding import PartitionSpec as P

HD = 128
TILE = 128
REACH = 2
PAIR = 2
OFFSETS = tuple(o for o in range(-REACH, REACH + 1) if o)
MASKED = -1e30
MESH = pl.DeviceIdType.MESH


def dot(a, b, contract):
    return lax.dot_general(a, b, (((1,), (contract,)), ((), ())), preferred_element_type=jnp.float32)


def kernel(devices, groups, chunk, lists, q, k, v, w, out,
           bias, packed, halo, ctx, ctx_mate, w_own, w_mate, part_out, part_in, own,
           halo_send, halo_recv, ctx_send, ctx_recv, part_send, part_recv, w_sems):
    device, group = lax.axis_index("ctx"), lax.axis_index("head")
    parity, place = group % 2, group // 2
    mate = group + 1 - 2 * parity
    tokens, columns = q.shape
    heads, tiles = columns // HD, tokens // TILE
    width = out.shape[1]
    rows = tokens // groups
    pairs = groups // 2
    chunks = width // chunk

    def reader(slot):
        return device - OFFSETS[slot]

    def source(slot):
        return device + OFFSETS[slot]

    def inside(index):
        return (index >= 0) & (index < devices)

    barrier = pltpu.get_barrier_semaphore()
    expected = jnp.int32(pairs)
    for slot in range(len(OFFSETS)):
        @pl.when(inside(reader(slot)))
        def _(slot=slot):
            pl.semaphore_signal(barrier, 1, device_id=(reader(slot), group), device_id_type=MESH)
        expected = expected + inside(source(slot)).astype(jnp.int32)
    pl.semaphore_signal(barrier, 1, device_id=(device, mate), device_id_type=MESH)
    for step in range(1, pairs):
        peer = 2 * ((place + step) % pairs) + parity
        pl.semaphore_signal(barrier, 1, device_id=(device, peer), device_id_type=MESH)

    load_w = pltpu.make_async_copy(w, w_own, w_sems.at[0])
    load_w.start()

    entries = lists.shape[0]

    def sent(r, found):
        found = list(found)
        for slot in range(len(OFFSETS)):
            row = (reader(slot) + devices) % devices * tiles + r
            for e in range(entries):
                x = lists[e, row] - device * tiles
                least, most = found[2 * slot], found[2 * slot + 1]
                found[2 * slot] = jnp.minimum(least, jnp.where(x < 0, tiles - 1, x))
                found[2 * slot + 1] = jnp.maximum(most, jnp.where(x >= tiles, 0, x))
        return tuple(found)

    ids = lax.fori_loop(0, tiles, sent, (jnp.int32(tiles - 1), jnp.int32(0)) * len(OFFSETS))

    for slot in range(len(OFFSETS)):
        for which in range(PAIR):
            picked = ids[PAIR * slot + which]
            for side, ref in ((0, k), (1, v)):
                tile = ref[picked]
                for h in range(heads):
                    packed[h, slot, side, which * TILE:(which + 1) * TILE, :] = tile[:, h * HD:(h + 1) * HD]
    for slot in range(len(OFFSETS)):
        @pl.when(jnp.logical_not(inside(source(slot))))
        def _(slot=slot):
            halo[:, :, slot] = jnp.zeros((heads, 2, PAIR * TILE, HD), halo.dtype)

    pl.semaphore_wait(barrier, expected)

    def halo_copy(h, slot):
        return pltpu.make_async_remote_copy(
            src_ref=packed.at[h, slot], dst_ref=halo.at[h, :, slot],
            send_sem=halo_send.at[h, slot], recv_sem=halo_recv.at[h, slot],
            device_id=(reader(slot), group), device_id_type=MESH)

    def each_send(act):
        def one(h, carry):
            for slot in range(len(OFFSETS)):
                @pl.when(inside(reader(slot)))
                def _(slot=slot):
                    act(halo_copy(h, slot))
            return carry
        lax.fori_loop(0, heads, one, 0)

    each_send(lambda copy: copy.start())
    send_w = pltpu.make_async_remote_copy(
        src_ref=w, dst_ref=w_mate, send_sem=w_sems.at[1], recv_sem=w_sems.at[2],
        device_id=(device, mate), device_id_type=MESH)
    send_w.start()

    def received(r, found):
        found = list(found)
        for e in range(entries):
            tile = lists[e, device * tiles + r]
            for slot in range(len(OFFSETS)):
                x = tile - source(slot) * tiles
                least, most = found[2 * slot], found[2 * slot + 1]
                found[2 * slot] = jnp.minimum(least, jnp.where(x < 0, tiles, x))
                found[2 * slot + 1] = jnp.maximum(most, jnp.where(x >= tiles, -1, x))
        return tuple(found)

    found = lax.fori_loop(0, tiles, received, (jnp.int32(tiles), jnp.int32(-1)) * len(OFFSETS))
    listed = [device * tiles + j for j in range(tiles)]
    for slot in range(len(OFFSETS)):
        least, most = found[2 * slot], found[2 * slot + 1]
        listed.append(jnp.where(least < tiles, source(slot) * tiles + least, -1))
        listed.append(jnp.where(most > least, source(slot) * tiles + most, -1))

    def mask(t, carry):
        added = [jnp.float32(MASKED)] * len(listed)
        for e in range(entries):
            tile = lists[e, device * tiles + t]
            added = [jnp.where(tile == other, 0.0, value) for other, value in zip(listed, added)]
        for j, value in enumerate(added):
            bias[t, :, j * TILE:(j + 1) * TILE] = jnp.full((1, TILE), value, jnp.float32)
        return carry

    lax.fori_loop(0, tiles, mask, 0)

    def ctx_copy(h, i):
        block = pl.multiple_of((2 * i + 1 - parity) * rows, rows)
        lanes = pl.ds(pl.multiple_of(h * HD, HD), HD)
        return pltpu.make_async_remote_copy(
            src_ref=ctx.at[pl.ds(block, rows), lanes],
            dst_ref=ctx_mate.at[pl.ds(i * rows, rows), lanes],
            send_sem=ctx_send.at[h, i], recv_sem=ctx_recv.at[h, i],
            device_id=(device, mate), device_id_type=MESH)

    scale = HD ** -0.5 * math.log2(math.e)
    near = tokens

    def one_head(h, carry):
        for slot in range(len(OFFSETS)):
            @pl.when(inside(source(slot)))
            def _(slot=slot):
                halo_copy(h, slot).wait_recv()
        lanes = pl.ds(pl.multiple_of(h * HD, HD), HD)
        k_own, v_own = k[:, :, lanes].reshape(tokens, HD), v[:, :, lanes].reshape(tokens, HD)
        k_far = halo[h, 0].reshape(len(OFFSETS) * PAIR * TILE, HD)
        v_far = halo[h, 1].reshape(len(OFFSETS) * PAIR * TILE, HD)
        for i in range(tiles):
            half = tiles // 2
            t = 2 * i + 1 - parity if i < half else 2 * (i - half) + parity
            span = pl.ds(pl.multiple_of(t * TILE, TILE), TILE)
            qt = q[span, lanes]
            shift = bias[t]
            s_own = dot(qt, k_own, 1) * scale + shift[:, :near]
            s_far = dot(qt, k_far, 1) * scale + shift[:, near:]
            top = jnp.maximum(jnp.max(s_own, axis=1, keepdims=True), jnp.max(s_far, axis=1, keepdims=True))
            p_own, p_far = jnp.exp2(s_own - top), jnp.exp2(s_far - top)
            total = jnp.sum(p_own, axis=1, keepdims=True) + jnp.sum(p_far, axis=1, keepdims=True)
            summed = dot(p_own.astype(jnp.bfloat16), v_own, 0) + dot(p_far.astype(jnp.bfloat16), v_far, 0)
            ctx[span, lanes] = (summed * (1.0 / total)).astype(ctx.dtype)
            if i == (half if rows == TILE and half < tiles else tiles - 1):
                for j in range(pairs):
                    ctx_copy(h, j).start()
        return carry

    lax.fori_loop(0, heads, one_head, 0)

    load_w.wait()
    send_w.wait_recv()

    def wait_ctx(h, carry):
        for j in range(pairs):
            ctx_copy(h, j).wait_recv()
        return carry
    lax.fori_loop(0, heads, wait_ctx, 0)

    def project(i, c):
        mine = ctx[pl.ds(pl.multiple_of((2 * i + parity) * rows, rows), rows), :]
        other = ctx_mate[pl.ds(pl.multiple_of(i * rows, rows), rows), :]
        cols = pl.ds(c * chunk, chunk)
        return dot(mine, w_own[:, cols], 0) + dot(other, w_mate[:, cols], 0)

    def part_copy(step, c):
        peer = 2 * ((place + step) % pairs) + parity
        cols = pl.ds(c * chunk, chunk)
        return pltpu.make_async_remote_copy(
            src_ref=part_out.at[step - 1, c], dst_ref=part_in.at[step - 1, c],
            send_sem=part_send.at[step - 1, c], recv_sem=part_recv.at[step - 1, c],
            device_id=(device, peer), device_id_type=MESH)

    waiting = None
    for step in range(1, pairs):
        for c in range(chunks):
            part_out[step - 1, c] = project((place + step) % pairs, c).astype(part_out.dtype)
            if waiting is not None:
                part_copy(*waiting).start()
            waiting = (step, c)
    for c in range(chunks):
        own[c] = project(place, c)
        if waiting is not None:
            part_copy(*waiting).start()
            waiting = None
    for c in range(chunks):
        total = own[c]
        for step in range(1, pairs):
            part_copy(step, c).wait_recv()
            total = total + part_in[step - 1, c].astype(jnp.float32)
        out[:, c * chunk:(c + 1) * chunk] = total.astype(out.dtype)

    each_send(lambda copy: copy.wait_send())
    send_w.wait_send()

    def drain_ctx(h, carry):
        for j in range(pairs):
            ctx_copy(h, j).wait_send()
        return carry
    lax.fori_loop(0, heads, drain_ctx, 0)
    for step in range(1, pairs):
        for c in range(chunks):
            part_copy(step, c).wait_send()


def body(queries, keys, values, kv_tiles, out_weight):
    tokens, columns = queries.shape
    width = out_weight.shape[1]
    devices, groups = lax.axis_size("ctx"), lax.axis_size("head")
    heads, rows, pairs, slots = columns // HD, tokens // groups, groups // 2, len(OFFSETS)
    chunk = min(width, 512)
    chunks = width // chunk
    vmem = pl.BlockSpec(memory_space=pltpu.VMEM)
    sems = pltpu.SemaphoreType.DMA
    bf16 = jnp.bfloat16
    return pl.pallas_call(
        functools.partial(kernel, devices, groups, chunk),
        out_shape=jax.ShapeDtypeStruct((rows, width), bf16),
        in_specs=[pl.BlockSpec(memory_space=pltpu.SMEM), vmem, vmem, vmem,
                  pl.BlockSpec(memory_space=pl.ANY)],
        out_specs=vmem,
        scratch_shapes=[
            pltpu.VMEM((tokens // TILE, 1, tokens + slots * PAIR * TILE), jnp.float32),
            pltpu.VMEM((heads, slots, 2, PAIR * TILE, HD), bf16),
            pltpu.VMEM((heads, 2, slots, PAIR * TILE, HD), bf16),
            pltpu.VMEM((tokens, columns), bf16),
            pltpu.VMEM((pairs * rows, columns), bf16),
            pltpu.VMEM((columns, width), bf16),
            pltpu.VMEM((columns, width), bf16),
            pltpu.VMEM((pairs - 1, chunks, rows, chunk), bf16),
            pltpu.VMEM((pairs - 1, chunks, rows, chunk), bf16),
            pltpu.VMEM((chunks, rows, chunk), jnp.float32),
            sems((heads, slots)), sems((heads, slots)),
            sems((heads, pairs)), sems((heads, pairs)),
            sems((pairs - 1, chunks)), sems((pairs - 1, chunks)),
            sems((3,)),
        ],
        compiler_params=pltpu.CompilerParams(
            collective_id=0, has_side_effects=True, vmem_limit_bytes=56 * 2 ** 20),
    )(kv_tiles.T, queries, keys.reshape(-1, TILE, columns), values.reshape(-1, TILE, columns), out_weight)


def solution(mesh):
    return jax.shard_map(
        body,
        mesh=mesh,
        in_specs=(P("ctx", "head"), P("ctx", "head"), P("ctx", "head"), P(), P("head", None)),
        out_specs=P(("ctx", "head"), None),
        check_vma=False,
    )
```

```python
import functools
import math

import jax
import jax.numpy as jnp
from jax import lax
from jax.experimental import pallas as pl
from jax.experimental.pallas import tpu as pltpu
from jax.sharding import PartitionSpec as P

HD = 128
TILE = 128
REACH = 2
PAIR = 2
OFFSETS = tuple(o for o in range(-REACH, REACH + 1) if o)
MASKED = -1e30
MESH = pl.DeviceIdType.MESH


def dot(a, b, contract):
    return lax.dot_general(a, b, (((1,), (contract,)), ((), ())), preferred_element_type=jnp.float32)


def kernel(devices, groups, chunk, lists, q, k, v, w, out,
           bias, packed, halo, ctx, ctx_mate, w_own, w_mate, part_out, part_in, own,
           halo_send, halo_recv, ctx_send, ctx_recv, part_send, part_recv, w_sems):
    device, group = lax.axis_index("ctx"), lax.axis_index("head")
    parity, place = group % 2, group // 2
    mate = group + 1 - 2 * parity
    tokens, columns = q.shape
    heads, tiles = columns // HD, tokens // TILE
    width = out.shape[1]
    rows = tokens // groups
    pairs = groups // 2
    chunks = width // chunk

    def reader(slot):
        return device - OFFSETS[slot]

    def source(slot):
        return device + OFFSETS[slot]

    def inside(index):
        return (index >= 0) & (index < devices)

    barrier = pltpu.get_barrier_semaphore()
    expected = jnp.int32(pairs)
    for slot in range(len(OFFSETS)):
        @pl.when(inside(reader(slot)))
        def _(slot=slot):
            pl.semaphore_signal(barrier, 1, device_id=(reader(slot), group), device_id_type=MESH)
        expected = expected + inside(source(slot)).astype(jnp.int32)
    pl.semaphore_signal(barrier, 1, device_id=(device, mate), device_id_type=MESH)
    for step in range(1, pairs):
        peer = 2 * ((place + step) % pairs) + parity
        pl.semaphore_signal(barrier, 1, device_id=(device, peer), device_id_type=MESH)

    load_w = pltpu.make_async_copy(w, w_own, w_sems.at[0])
    load_w.start()

    entries = lists.shape[0]

    def sent(r, found):
        found = list(found)
        for slot in range(len(OFFSETS)):
            row = (reader(slot) + devices) % devices * tiles + r
            for e in range(entries):
                x = lists[e, row] - device * tiles
                least, most = found[2 * slot], found[2 * slot + 1]
                found[2 * slot] = jnp.minimum(least, jnp.where(x < 0, tiles - 1, x))
                found[2 * slot + 1] = jnp.maximum(most, jnp.where(x >= tiles, 0, x))
        return tuple(found)

    ids = lax.fori_loop(0, tiles, sent, (jnp.int32(tiles - 1), jnp.int32(0)) * len(OFFSETS))

    def pack(h):
        for slot in range(len(OFFSETS)):
            for which in range(PAIR):
                for side, ref in ((0, k), (1, v)):
                    tile = ref[ids[PAIR * slot + which]]
                    packed[h, slot, side, which * TILE:(which + 1) * TILE, :] = tile[:, h * HD:(h + 1) * HD]

    pack(0)
    for slot in range(len(OFFSETS)):
        @pl.when(jnp.logical_not(inside(source(slot))))
        def _(slot=slot):
            halo[:, :, slot] = jnp.zeros((heads, 2, PAIR * TILE, HD), halo.dtype)

    pl.semaphore_wait(barrier, expected)

    def halo_copy(h, slot):
        return pltpu.make_async_remote_copy(
            src_ref=packed.at[h, slot], dst_ref=halo.at[h, :, slot],
            send_sem=halo_send.at[h, slot], recv_sem=halo_recv.at[h, slot],
            device_id=(reader(slot), group), device_id_type=MESH)

    def send(h, act):
        for slot in range(len(OFFSETS)):
            @pl.when(inside(reader(slot)))
            def _(slot=slot):
                act(halo_copy(h, slot))

    for h in range(heads):
        if h + 1 < heads:
            pack(h + 1)
        send(h, lambda copy: copy.start())
    send_w = pltpu.make_async_remote_copy(
        src_ref=w, dst_ref=w_mate, send_sem=w_sems.at[1], recv_sem=w_sems.at[2],
        device_id=(device, mate), device_id_type=MESH)
    send_w.start()

    def received(r, found):
        found = list(found)
        for e in range(entries):
            tile = lists[e, device * tiles + r]
            for slot in range(len(OFFSETS)):
                x = tile - source(slot) * tiles
                least, most = found[2 * slot], found[2 * slot + 1]
                found[2 * slot] = jnp.minimum(least, jnp.where(x < 0, tiles, x))
                found[2 * slot + 1] = jnp.maximum(most, jnp.where(x >= tiles, -1, x))
        return tuple(found)

    found = lax.fori_loop(0, tiles, received, (jnp.int32(tiles), jnp.int32(-1)) * len(OFFSETS))
    listed = [device * tiles + j for j in range(tiles)]
    for slot in range(len(OFFSETS)):
        least, most = found[2 * slot], found[2 * slot + 1]
        listed.append(jnp.where(least < tiles, source(slot) * tiles + least, -1))
        listed.append(jnp.where(most > least, source(slot) * tiles + most, -1))

    def mask(t, carry):
        added = [jnp.float32(MASKED)] * len(listed)
        for e in range(entries):
            tile = lists[e, device * tiles + t]
            added = [jnp.where(tile == other, 0.0, value) for other, value in zip(listed, added)]
        for j, value in enumerate(added):
            bias[t, :, j * TILE:(j + 1) * TILE] = jnp.full((1, TILE), value, jnp.float32)
        return carry

    lax.fori_loop(0, tiles, mask, 0)

    def ctx_copy(h, i):
        block = pl.multiple_of((2 * i + 1 - parity) * rows, rows)
        lanes = pl.ds(pl.multiple_of(h * HD, HD), HD)
        return pltpu.make_async_remote_copy(
            src_ref=ctx.at[pl.ds(block, rows), lanes],
            dst_ref=ctx_mate.at[pl.ds(i * rows, rows), lanes],
            send_sem=ctx_send.at[h, i], recv_sem=ctx_recv.at[h, i],
            device_id=(device, mate), device_id_type=MESH)

    scale = HD ** -0.5 * math.log2(math.e)
    near = tokens

    def one_head(h, carry):
        for slot in range(len(OFFSETS)):
            @pl.when(inside(source(slot)))
            def _(slot=slot):
                halo_copy(h, slot).wait_recv()
        lanes = pl.ds(pl.multiple_of(h * HD, HD), HD)
        k_own, v_own = k[:, :, lanes].reshape(tokens, HD), v[:, :, lanes].reshape(tokens, HD)
        k_far = halo[h, 0].reshape(len(OFFSETS) * PAIR * TILE, HD)
        v_far = halo[h, 1].reshape(len(OFFSETS) * PAIR * TILE, HD)
        for i in range(tiles):
            half = tiles // 2
            t = 2 * i + 1 - parity if i < half else 2 * (i - half) + parity
            span = pl.ds(pl.multiple_of(t * TILE, TILE), TILE)
            qt = q[span, lanes]
            shift = bias[t]
            s_own = dot(qt, k_own, 1) * scale + shift[:, :near]
            s_far = dot(qt, k_far, 1) * scale + shift[:, near:]
            top = jnp.maximum(jnp.max(s_own, axis=1, keepdims=True), jnp.max(s_far, axis=1, keepdims=True))
            p_own, p_far = jnp.exp2(s_own - top), jnp.exp2(s_far - top)
            total = jnp.sum(p_own, axis=1, keepdims=True) + jnp.sum(p_far, axis=1, keepdims=True)
            summed = dot(p_own.astype(jnp.bfloat16), v_own, 0) + dot(p_far.astype(jnp.bfloat16), v_far, 0)
            ctx[span, lanes] = (summed * (1.0 / total)).astype(ctx.dtype)
            if i == (half if rows == TILE and half < tiles else tiles - 1):
                for j in range(pairs):
                    ctx_copy(h, j).start()
        return carry

    lax.fori_loop(0, heads, one_head, 0)

    load_w.wait()
    send_w.wait_recv()

    def wait_ctx(h, carry):
        for j in range(pairs):
            ctx_copy(h, j).wait_recv()
        return carry
    lax.fori_loop(0, heads, wait_ctx, 0)

    def project(i, c):
        mine = ctx[pl.ds(pl.multiple_of((2 * i + parity) * rows, rows), rows), :]
        other = ctx_mate[pl.ds(pl.multiple_of(i * rows, rows), rows), :]
        cols = pl.ds(c * chunk, chunk)
        return dot(mine, w_own[:, cols], 0) + dot(other, w_mate[:, cols], 0)

    def part_copy(step, c):
        peer = 2 * ((place + step) % pairs) + parity
        cols = pl.ds(c * chunk, chunk)
        return pltpu.make_async_remote_copy(
            src_ref=part_out.at[step - 1, c], dst_ref=part_in.at[step - 1, c],
            send_sem=part_send.at[step - 1, c], recv_sem=part_recv.at[step - 1, c],
            device_id=(device, peer), device_id_type=MESH)

    waiting = None
    for step in range(1, pairs):
        for c in range(chunks):
            part_out[step - 1, c] = project((place + step) % pairs, c).astype(part_out.dtype)
            if waiting is not None:
                part_copy(*waiting).start()
            waiting = (step, c)
    for c in range(chunks):
        own[c] = project(place, c)
        if waiting is not None:
            part_copy(*waiting).start()
            waiting = None
    for c in range(chunks):
        total = own[c]
        for step in range(1, pairs):
            part_copy(step, c).wait_recv()
            total = total + part_in[step - 1, c].astype(jnp.float32)
        out[:, c * chunk:(c + 1) * chunk] = total.astype(out.dtype)

    def drain_halo(h, carry):
        send(h, lambda copy: copy.wait_send())
        return carry
    lax.fori_loop(0, heads, drain_halo, 0)
    send_w.wait_send()

    def drain_ctx(h, carry):
        for j in range(pairs):
            ctx_copy(h, j).wait_send()
        return carry
    lax.fori_loop(0, heads, drain_ctx, 0)
    for step in range(1, pairs):
        for c in range(chunks):
            part_copy(step, c).wait_send()


def body(queries, keys, values, kv_tiles, out_weight):
    tokens, columns = queries.shape
    width = out_weight.shape[1]
    devices, groups = lax.axis_size("ctx"), lax.axis_size("head")
    heads, rows, pairs, slots = columns // HD, tokens // groups, groups // 2, len(OFFSETS)
    chunk = min(width, 256)
    chunks = width // chunk
    vmem = pl.BlockSpec(memory_space=pltpu.VMEM)
    sems = pltpu.SemaphoreType.DMA
    bf16 = jnp.bfloat16
    return pl.pallas_call(
        functools.partial(kernel, devices, groups, chunk),
        out_shape=jax.ShapeDtypeStruct((rows, width), bf16),
        in_specs=[pl.BlockSpec(memory_space=pltpu.SMEM), vmem, vmem, vmem,
                  pl.BlockSpec(memory_space=pl.ANY)],
        out_specs=vmem,
        scratch_shapes=[
            pltpu.VMEM((tokens // TILE, 1, tokens + slots * PAIR * TILE), jnp.float32),
            pltpu.VMEM((heads, slots, 2, PAIR * TILE, HD), bf16),
            pltpu.VMEM((heads, 2, slots, PAIR * TILE, HD), bf16),
            pltpu.VMEM((tokens, columns), bf16),
            pltpu.VMEM((pairs * rows, columns), bf16),
            pltpu.VMEM((columns, width), bf16),
            pltpu.VMEM((columns, width), bf16),
            pltpu.VMEM((pairs - 1, chunks, rows, chunk), bf16),
            pltpu.VMEM((pairs - 1, chunks, rows, chunk), bf16),
            pltpu.VMEM((chunks, rows, chunk), jnp.float32),
            sems((heads, slots)), sems((heads, slots)),
            sems((heads, pairs)), sems((heads, pairs)),
            sems((pairs - 1, chunks)), sems((pairs - 1, chunks)),
            sems((3,)),
        ],
        compiler_params=pltpu.CompilerParams(
            collective_id=0, has_side_effects=True, vmem_limit_bytes=56 * 2 ** 20),
    )(kv_tiles.T, queries, keys.reshape(-1, TILE, columns), values.reshape(-1, TILE, columns), out_weight)


def solution(mesh):
    return jax.shard_map(
        body,
        mesh=mesh,
        in_specs=(P("ctx", "head"), P("ctx", "head"), P("ctx", "head"), P(), P("head", None)),
        out_specs=P(("ctx", "head"), None),
        check_vma=False,
    )
```
